256 devices in a mesh: blk: 32 (over z, x_hi, core), shell: 8 (over x_lo, y).
Axes of the slice: x: 4 (x_hi: 2, x_lo: 2; x = x_hi * 2 + x_lo), y: 4, z: 8, core: 2. Of those that a mesh axis runs over, the one named last changes fastest.
Arguments:
- spectra: bfloat16 [128, 8, 256, 2048], P(None, None, 'shell', 'blk'), may hold values from -6 to 6
- selection: float32 [256, 2048], P('shell', 'blk'), may hold values from 0.3 to 3
- legendre: bfloat16 [64, 2048, 1024], P('blk'), may hold values from -0.125 to 0.125
- bessel: bfloat16 [1024, 128, 256], P(('blk', 'shell')), may hold values from -0.375 to 0.375
- order_perm: int32 [64], replicated, may hold values from 0 to 63, each once
Outputs:
- coeffs: float32 [1024, 8, 128, 128], P(('blk', 'shell'))
The draws below stay inside these ranges and needn't reach their ends.
Inputs may be any that keep to these rules, and one draw needn't show every extreme that they name: `order_perm`: each order slot holds a different order.
All inputs are finite; a program needn't handle non-finite values.
Results may differ from the reference program's by a relative error of at most 0.0041.
Values may be sent and summed in bfloat16 or wider, within the bound.
No kernel may reach another device: no remote copies, remote signals or barrier semaphores. Data moves between devices by JAX's collectives and lax.ppermute only.
A program may use at most 128 MiB of HBM per device.

```python
import math
import jax
import jax.numpy as jnp
from jax import lax

CYCLES = 2048
SHELLS = 256
DEGREES = 1024
KMODES = 128
FIELDS = 8
ORDERS = 64


def block_levels(stream_key, extent, shards, low, largest):
    gain = 1.0
    for axis_at, shards_of in shards:
        steps = jax.random.uniform(jax.random.fold_in(jax.random.fold_in(stream_key, 6), axis_at), (shards_of,), jnp.float32, low / len(shards), largest / len(shards))
        gain = gain * jnp.repeat(jnp.exp(steps), extent[axis_at] // shards_of).reshape((-1,) + (1,) * (len(extent) - 1 - axis_at))
    return gain


def bell_draw(key, dims, width, limit, shards=(), kind=jnp.bfloat16):
    array = jax.random.normal(key, dims, jnp.float32) * width
    if len(shards) > 0:
        array = block_levels(key, dims, shards, -0.22, 0.18) * array
    return jnp.clip(array, min=-limit, max=limit).astype(kind)


def setup_inputs(seed: int = 0) -> dict:
    key_list = jax.random.split(jax.random.key(seed), 6)
    return {
        "spectra": bell_draw(key_list[0], (2 * ORDERS, FIELDS, SHELLS, CYCLES), 1.0, 6.0, ((2, 8), (3, 32))),
        "selection": jnp.clip(jnp.exp(math.log(3.0) - 2.3025851 * jax.random.uniform(key_list[1], (SHELLS, CYCLES), jnp.float32) ** block_levels(key_list[1], (SHELLS, CYCLES), ((0, 8), (1, 32)), -0.2, 0.2)), 0.3, 3.0),
        "legendre": bell_draw(key_list[2], (ORDERS, CYCLES, DEGREES), CYCLES ** -0.5, 0.125, ((0, 32),)),
        "bessel": bell_draw(key_list[3], (DEGREES, KMODES, SHELLS), SHELLS ** -0.5, 0.375, ((0, 256),)),
        "order_perm": jax.random.permutation(key_list[4], ORDERS).astype(jnp.int32),
    }


def reference(spectra, selection, legendre, bessel, order_perm):
    column_pairs = (2 * order_perm[:, None] + jnp.arange(2, dtype=jnp.int32)[None, :]).astype(jnp.int32)

    def one_order(packed):
        legendre_rows, column_pair = packed
        picked = jnp.take(spectra, column_pair, axis=0).astype(jnp.float32)
        weighted = (picked * selection[None, None, :, :]).astype(jnp.bfloat16).astype(jnp.float32)
        product = jnp.einsum("cfsj,jl->lfcs", weighted, legendre_rows.astype(jnp.float32))
        return product.astype(jnp.bfloat16)

    per_order = lax.map(one_order, (legendre, column_pairs))
    degree_count = per_order.shape[1]
    field_count = per_order.shape[2]
    shell_count = per_order.shape[4]
    harmonic = jnp.transpose(per_order, (1, 2, 0, 3, 4)).reshape(degree_count, field_count, -1, shell_count)

    def one_degree(packed):
        degree_rows, bessel_rows = packed
        return jnp.einsum("fxs,ks->fxk", degree_rows.astype(jnp.float32), bessel_rows.astype(jnp.float32))

    return lax.map(one_degree, (harmonic, bessel))
```

```python
import functools
import jax
import jax.numpy as jnp
from jax import lax
from jax.experimental import pallas as pl
from jax.experimental.pallas import tpu as pltpu
from jax.sharding import PartitionSpec as P

NT = (((1,), (1,)), ((), ()))
NN = (((1,), (0,)), ((), ()))


def weigh_kernel(perm_ref, sel_ref, x_ref, o_ref, scr):
    slot = lax.broadcasted_iota(jnp.int32, (128, 64), 0) // 2
    lane = lax.broadcasted_iota(jnp.int32, (128, 64), 1)
    held = jnp.sum(jnp.where(slot == lane, perm_ref[...], 0), axis=1, keepdims=True)
    row = lax.broadcasted_iota(jnp.int32, (128, 128), 0)
    col = lax.broadcasted_iota(jnp.int32, (128, 128), 1)
    pick = jnp.where(2 * held + row % 2 == col, 1.0, 0.0).astype(jnp.bfloat16)
    for g in range(8):
        y = lax.dot_general(
            pick, x_ref[0, g * 256 : (g + 1) * 256, :], NT, preferred_element_type=jnp.float32
        )
        for h in range(2):
            rp = 2 * g + h
            scr[pl.ds(rp, 128, stride=16), :] = y[:, h * 128 : (h + 1) * 128] * sel_ref[rp : rp + 1, :]
    o_ref[:, 0, :, :] = scr[...].reshape(128, 16, 128).astype(jnp.bfloat16)


def weigh(perm, sel, x, half):
    return pl.pallas_call(
        weigh_kernel,
        grid=(4,),
        in_specs=[
            pl.BlockSpec((1, 64), lambda i: (0, 0)),
            pl.BlockSpec((16, 128), lambda i: (0, 0)),
            pl.BlockSpec((1, 2048, 128), lambda i: (4 * half + i, 0, 0)),
        ],
        out_specs=pl.BlockSpec((128, 1, 16, 128), lambda i: (0, i, 0, 0)),
        out_shape=jax.ShapeDtypeStruct((128, 4, 16, 128), jnp.bfloat16),
        scratch_shapes=[pltpu.VMEM((2048, 128), jnp.float32)],
        name="weigh",
        cost_estimate=pl.CostEstimate(flops=2 * 8192 * 128 * 128, bytes_accessed=4 << 20, transcendentals=0),
    )(perm, sel, x)


LT = 256


def angular_kernel(r_ref, leg_ref, o_ref, lhs, scr):
    @pl.when(pl.program_id(0) == 0)
    def _():
        for p in range(4):
            s, c = p // 2, p % 2
            for g in range(16):
                a = r_ref[2 * g, p * 64 : (p + 1) * 64, :]
                b = r_ref[2 * g + 1, p * 64 : (p + 1) * 64, :]
                ks = slice(g * 128, (g + 1) * 128)
                lhs[s, c * 128 : c * 128 + 64, ks] = jnp.concatenate([a[:, :64], b[:, :64]], axis=1)
                lhs[s, c * 128 + 64 : c * 128 + 128, ks] = jnp.concatenate([a[:, 64:], b[:, 64:]], axis=1)

    for s in range(2):
        h = lax.dot_general(lhs[s], leg_ref[s], NN, preferred_element_type=jnp.float32)
        ht = h.T
        for c in range(2):
            scr[pl.ds(2 * s + c, LT, stride=4), :] = ht[:, c * 128 : (c + 1) * 128]
    o_ref[...] = scr[...].astype(jnp.bfloat16)


def angular(r, leg):
    return pl.pallas_call(
        angular_kernel,
        grid=(1024 // LT,),
        in_specs=[
            pl.BlockSpec(memory_space=pltpu.VMEM),
            pl.BlockSpec((2, 2048, LT), lambda i: (0, 0, i)),
        ],
        out_specs=pl.BlockSpec((LT * 4, 128), lambda i: (i, 0)),
        out_shape=jax.ShapeDtypeStruct((4096, 128), jnp.bfloat16),
        scratch_shapes=[pltpu.VMEM((2, 256, 2048), jnp.bfloat16), pltpu.VMEM((LT * 4, 128), jnp.float32)],
        name="angular",
        cost_estimate=pl.CostEstimate(flops=2 * 512 * 2048 * 1024, bytes_accessed=11 << 20, transcendentals=0),
    )(r, leg)


def radial_kernel(r_ref, bes_ref, *rest):
    o_ref, wide, spread, weight = rest[-4:]
    l = pl.program_id(0)

    @pl.when(l == 0)
    def _():
        wide[...] = r_ref[...].astype(jnp.float32)
        src = lax.broadcasted_iota(jnp.int32, (256, 1024), 0)
        lam = lax.broadcasted_iota(jnp.int32, (256, 1024), 1)
        shell = (lam // 128) * 32 + 2 * (lam % 16) + (lam // 64) % 2
        spread[...] = jnp.where(src == shell, 1.0, 0.0).astype(jnp.bfloat16)

    tiled = lax.dot_general(bes_ref[0], spread[...], NN, preferred_element_type=jnp.float32)
    field = (lax.broadcasted_iota(jnp.int32, (128, 1024), 1) // 16) % 4
    for f in range(4):
        weight[f * 128 : (f + 1) * 128, :] = jnp.where(field == f, tiled, 0.0).astype(jnp.bfloat16)
    lhs = jnp.concatenate(
        [
            jnp.concatenate([wide[pl.ds(l * 4 + q * 16 + p, 32, stride=128), :] for p in range(4)], axis=0)
            for q in range(8)
        ],
        axis=1,
    ).astype(jnp.bfloat16)
    y = lax.dot_general(lhs, weight[...], NT, preferred_element_type=jnp.float32)
    for f in range(4):
        for p in range(4):
            o_ref[0, f, pl.ds(p, 32, stride=4), :] = y[p * 32 : (p + 1) * 32, f * 128 : (f + 1) * 128]


def radial(r, bes, half, prior):
    more = () if prior is None else (prior,)
    return pl.pallas_call(
        radial_kernel,
        grid=(4,),
        in_specs=[
            pl.BlockSpec(memory_space=pltpu.VMEM),
            pl.BlockSpec((1, 128, 256), lambda i: (i, 0, 0)),
        ]
        + [pl.BlockSpec(memory_space=pl.ANY)] * len(more),
        out_specs=pl.BlockSpec((1, 4, 128, 128), lambda i: (i, half, 0, 0)),
        out_shape=jax.ShapeDtypeStruct((4, 8, 128, 128), jnp.float32),
        scratch_shapes=[
            pltpu.VMEM((4096, 128), jnp.float32),
            pltpu.VMEM((256, 1024), jnp.bfloat16),
            pltpu.VMEM((512, 1024), jnp.bfloat16),
        ],
        input_output_aliases={2: 0} if more else {},
        name="radial",
        cost_estimate=pl.CostEstimate(flops=2 * 4 * 128 * 1024 * 512, bytes_accessed=3 << 20, transcendentals=0),
    )(r, bes, *more)


def on_device(spectra, selection, legendre, bessel, order_perm):
    x = jnp.transpose(spectra, (1, 2, 3, 0)).reshape(8, 2048, 128)
    sel = selection.reshape(16, 128)
    perm = order_perm.reshape(1, 64)
    out = None
    for half in range(2):
        w = weigh(perm, sel, x, half).reshape(32, 256, 128)
        w = lax.all_to_all(w, "blk", split_axis=0, concat_axis=0, tiled=True)
        h = angular(w, legendre).reshape(256, 16, 128)
        h = lax.all_to_all(h, ("blk", "shell"), split_axis=0, concat_axis=0, tiled=True)
        out = radial(h.reshape(4096, 128), bessel, half, out)
    return out


def solution(mesh):
    in_specs = (
        P(None, None, "shell", "blk"),
        P("shell", "blk"),
        P("blk", None, None),
        P(("blk", "shell"), None, None),
        P(),
    )
    out_specs = P(("blk", "shell"), None, None, None)
    return jax.shard_map(
        on_device, mesh=mesh, in_specs=in_specs, out_specs=out_specs, check_vma=False
    )
```

```python
import functools
import jax
import jax.numpy as jnp
from jax import lax
from jax.experimental import pallas as pl
from jax.experimental.pallas import tpu as pltpu
from jax.sharding import PartitionSpec as P

NT = (((1,), (1,)), ((), ()))
NN = (((1,), (0,)), ((), ()))
BF = jnp.bfloat16
F32 = jnp.float32
WHOLE = pl.BlockSpec(memory_space=pltpu.VMEM)


def cost(flops, moved):
    return pl.CostEstimate(flops=flops, bytes_accessed=moved, transcendentals=0)


PITCH = 16


def weigh_kernel(perm_ref, sel_ref, x_ref, o_ref, scr):
    p = lax.broadcasted_iota(jnp.int32, (128, 64), 0)
    lane = lax.broadcasted_iota(jnp.int32, (128, 64), 1)
    held = jnp.sum(jnp.where(p // 2 == lane, 2 * perm_ref[...] + p % 2, 0), axis=1, keepdims=True)
    col = lax.broadcasted_iota(jnp.int32, (128, 128), 1)
    pick = jnp.where(held == col, 1.0, 0.0).astype(BF)
    for g in range(8):
        y = lax.dot_general(pick, x_ref[0, g * 256 : (g + 1) * 256, :], NT, preferred_element_type=F32)
        for h in range(2):
            rp = 2 * g + h
            scr[pl.ds(rp, 128, stride=PITCH), :] = y[:, h * 128 : (h + 1) * 128] * sel_ref[rp : rp + 1, :]
    if PITCH == 16:
        o_ref[:, 0, :, :] = scr[...].reshape(128, 16, 128).astype(BF)
    else:
        for q in range(128):
            o_ref[q, 0, :, :] = scr[q * PITCH : q * PITCH + 16, :].astype(BF)


def weigh(perm, sel, x):
    return pl.pallas_call(
        weigh_kernel,
        grid=(8,),
        in_specs=[
            pl.BlockSpec((1, 64), lambda i: (0, 0)),
            pl.BlockSpec((16, 128), lambda i: (0, 0)),
            pl.BlockSpec((1, 2048, 128), lambda i: (i, 0, 0)),
        ],
        out_specs=pl.BlockSpec((128, 1, 16, 128), lambda i: (0, i, 0, 0)),
        out_shape=jax.ShapeDtypeStruct((128, 8, 16, 128), BF),
        scratch_shapes=[pltpu.VMEM((128 * PITCH, 128), F32)],
        name="weigh",
        cost_estimate=cost(2 * 16384 * 128 * 128, 8 << 20),
    )(perm, sel, x)


LT = 256
LP = 8


def angular_kernel(r_ref, leg_ref, o_ref, lhs, scr):
    @pl.when(pl.program_id(0) == 0)
    def _():
        for p in range(4):
            s, c = p // 2, p % 2
            for fh in range(2):
                rows = slice(p * 128 + fh * 64, p * 128 + fh * 64 + 64)
                to = c * 256 + fh * 128
                for g in range(16):
                    a = r_ref[2 * g, rows, :]
                    b = r_ref[2 * g + 1, rows, :]
                    ks = slice(g * 128, (g + 1) * 128)
                    lhs[s, to : to + 64, ks] = jnp.concatenate([a[:, :64], b[:, :64]], axis=1)
                    lhs[s, to + 64 : to + 128, ks] = jnp.concatenate([a[:, 64:], b[:, 64:]], axis=1)

    for s in range(2):
        h = lax.dot_general(lhs[s], leg_ref[s], NN, preferred_element_type=F32)
        ht = h.T
        for n in range(4):
            scr[pl.ds(4 * s + n, LT, stride=LP), :] = ht[:, n * 128 : (n + 1) * 128]
    if LP == 8:
        o_ref[...] = scr[...].astype(BF)
    else:
        for l in range(0, LT, 2):
            o_ref[l * 8 : l * 8 + 16, :] = jnp.concatenate(
                [scr[l * LP : l * LP + 8, :], scr[(l + 1) * LP : (l + 1) * LP + 8, :]], axis=0
            ).astype(BF)


def angular(r, leg):
    return pl.pallas_call(
        angular_kernel,
        grid=(1024 // LT,),
        in_specs=[WHOLE, pl.BlockSpec((2, 2048, LT), lambda i: (0, 0, i))],
        out_specs=pl.BlockSpec((LT * 8, 128), lambda i: (i, 0)),
        out_shape=jax.ShapeDtypeStruct((8192, 128), BF),
        scratch_shapes=[pltpu.VMEM((2, 512, 2048), BF), pltpu.VMEM((LT * LP, 128), F32)],
        name="angular",
        cost_estimate=cost(2 * 1024 * 2048 * 1024, 14 << 20),
    )(r, leg)


def spread_kernel(bes_ref, o_ref):
    src = lax.broadcasted_iota(jnp.int32, (256, 1024), 0)
    lam = lax.broadcasted_iota(jnp.int32, (256, 1024), 1)
    shell = (lam // 128) * 32 + 2 * (lam % 16) + (lam // 64) % 2
    one = jnp.where(src == shell, 1.0, 0.0).astype(BF)
    o_ref[...] = lax.dot_general(bes_ref[...], one, NN, preferred_element_type=F32).astype(BF)


def spread(bes):
    return pl.pallas_call(
        spread_kernel,
        in_specs=[WHOLE],
        out_specs=WHOLE,
        out_shape=jax.ShapeDtypeStruct((512, 1024), BF),
        name="spread",
        cost_estimate=cost(2 * 512 * 256 * 1024, 2 << 20),
    )(bes)


def radial_kernel(r_ref, wide_ref, o_ref, f32s, weight, held):
    l = pl.program_id(0)

    @pl.when(l == 0)
    def _():
        f32s[...] = r_ref[...].astype(F32)

    field = (lax.broadcasted_iota(jnp.int32, (128, 1024), 1) // 16) % 4
    tiled = wide_ref[...]
    for f in range(4):
        weight[f * 128 : (f + 1) * 128, :] = jnp.where(field == f, tiled, jnp.zeros_like(tiled))
    for n in range(8):
        for q in range(8):
            held[n * 32 : (n + 1) * 32, q * 128 : (q + 1) * 128] = f32s[
                pl.ds(q * 32 + l * 8 + n, 32, stride=256), :
            ].astype(BF)
    y = lax.dot_general(held[...], weight[...], NT, preferred_element_type=F32)
    for n in range(8):
        p, fh = n // 2, n % 2
        for f in range(4):
            o_ref[0, fh * 4 + f, pl.ds(p, 32, stride=4), :] = y[n * 32 : (n + 1) * 32, f * 128 : (f + 1) * 128]


def radial(r, wide):
    return pl.pallas_call(
        radial_kernel,
        grid=(4,),
        in_specs=[WHOLE, pl.BlockSpec((128, 1024), lambda i: (i, 0))],
        out_specs=pl.BlockSpec((1, 8, 128, 128), lambda i: (i, 0, 0, 0)),
        out_shape=jax.ShapeDtypeStruct((4, 8, 128, 128), F32),
        scratch_shapes=[pltpu.VMEM((8192, 128), F32), pltpu.VMEM((512, 1024), BF), pltpu.VMEM((256, 1024), BF)],
        name="radial",
        cost_estimate=cost(2 * 4 * 256 * 1024 * 512, 5 << 20),
    )(r, wide)


def on_device(spectra, selection, legendre, bessel, order_perm):
    x = jnp.transpose(spectra, (1, 2, 3, 0)).reshape(8, 2048, 128)
    w = weigh(order_perm.reshape(1, 64), selection.reshape(16, 128), x).reshape(32, 512, 128)
    w = lax.all_to_all(w, "blk", split_axis=0, concat_axis=0, tiled=True)
    wide = spread(bessel.reshape(512, 256))
    h = angular(w, legendre).reshape(256, 32, 128)
    h = lax.all_to_all(h, ("blk", "shell"), split_axis=0, concat_axis=0, tiled=True)
    return radial(h.reshape(8192, 128), wide)


def solution(mesh):
    in_specs = (
        P(None, None, "shell", "blk"),
        P("shell", "blk"),
        P("blk", None, None),
        P(("blk", "shell"), None, None),
        P(),
    )
    out_specs = P(("blk", "shell"), None, None, None)
    return jax.shard_map(
        on_device, mesh=mesh, in_specs=in_specs, out_specs=out_specs, check_vma=False
    )
```

```python
import functools
import jax
import jax.numpy as jnp
from jax import lax
from jax.experimental import pallas as pl
from jax.experimental.pallas import tpu as pltpu
from jax.sharding import PartitionSpec as P

NT = (((1,), (1,)), ((), ()))
NN = (((1,), (0,)), ((), ()))
BF = jnp.bfloat16
F32 = jnp.float32
WHOLE = pl.BlockSpec(memory_space=pltpu.VMEM)


def cost(flops, moved):
    return pl.CostEstimate(flops=flops, bytes_accessed=moved, transcendentals=0)


RAWSEL = True
PITCH = 16


def weigh_kernel(perm_ref, sel_ref, x_ref, o_ref, scr, pair):
    @pl.when(pl.program_id(0) == 0)
    def _():
        for rp in range(16):
            pair[rp : rp + 1, :] = jnp.concatenate(
                [sel_ref[2 * rp : 2 * rp + 1, :], sel_ref[2 * rp + 1 : 2 * rp + 2, :]], axis=1
            )

    p = lax.broadcasted_iota(jnp.int32, (128, 64), 0)
    lane = lax.broadcasted_iota(jnp.int32, (128, 64), 1)
    held = jnp.sum(jnp.where(p // 2 == lane, 2 * perm_ref[...] + p % 2, 0), axis=1, keepdims=True)
    col = lax.broadcasted_iota(jnp.int32, (128, 128), 1)
    pick = jnp.where(held == col, 1.0, 0.0).astype(BF)
    for g in range(8):
        y = lax.dot_general(pick, x_ref[0, g * 256 : (g + 1) * 256, :], NT, preferred_element_type=F32)
        for h in range(2):
            rp = 2 * g + h
            scr[pl.ds(rp, 128, stride=PITCH), :] = y[:, h * 128 : (h + 1) * 128] * pair[rp : rp + 1, :]
    if PITCH == 16:
        o_ref[:, 0, :, :] = scr[...].reshape(128, 16, 128).astype(BF)
    else:
        for q in range(128):
            o_ref[q, 0, :, :] = scr[q * PITCH : q * PITCH + 16, :].astype(BF)


def weigh(perm, sel, x):
    return pl.pallas_call(
        weigh_kernel,
        grid=(8,),
        in_specs=[
            pl.BlockSpec((1, 64), lambda i: (0, 0)),
            pl.BlockSpec((32, 64), lambda i: (0, 0)),
            pl.BlockSpec((1, 2048, 128), lambda i: (i, 0, 0)),
        ],
        out_specs=pl.BlockSpec((128, 1, 16, 128), lambda i: (0, i, 0, 0)),
        out_shape=jax.ShapeDtypeStruct((128, 8, 16, 128), BF),
        scratch_shapes=[pltpu.VMEM((128 * PITCH, 128), F32), pltpu.VMEM((16, 128), F32)],
        name="weigh",
        compiler_params=pltpu.CompilerParams(vmem_limit_bytes=8 << 20),
        cost_estimate=cost(2 * 16384 * 128 * 128, 8 << 20),
    )(perm, sel, x)


LT = 256
LP = 8


def angular_kernel(r_ref, leg_ref, o_ref, lhs, scr):
    @pl.when(pl.program_id(0) == 0)
    def _():
        for p in range(4):
            s, c = p // 2, p % 2
            for fh in range(2):
                rows = slice(p * 128 + fh * 64, p * 128 + fh * 64 + 64)
                to = c * 256 + fh * 128
                for g in range(16):
                    a = r_ref[2 * g, rows, :]
                    b = r_ref[2 * g + 1, rows, :]
                    ks = slice(g * 128, (g + 1) * 128)
                    lhs[s, to : to + 64, ks] = jnp.concatenate([a[:, :64], b[:, :64]], axis=1)
                    lhs[s, to + 64 : to + 128, ks] = jnp.concatenate([a[:, 64:], b[:, 64:]], axis=1)

    for s in range(2):
        h = lax.dot_general(lhs[s], leg_ref[s, :, pl.ds(pl.multiple_of(pl.program_id(0) * LT, LT), LT)], NN, preferred_element_type=F32)
        ht = h.T
        for n in range(4):
            scr[pl.ds(4 * s + n, LT, stride=LP), :] = ht[:, n * 128 : (n + 1) * 128]
    if LP == 8:
        o_ref[...] = scr[...].astype(BF)
    else:
        for l in range(0, LT, 2):
            o_ref[l * 8 : l * 8 + 16, :] = jnp.concatenate(
                [scr[l * LP : l * LP + 8, :], scr[(l + 1) * LP : (l + 1) * LP + 8, :]], axis=0
            ).astype(BF)


def angular(r, leg):
    return pl.pallas_call(
        angular_kernel,
        grid=(1024 // LT,),
        in_specs=[WHOLE, WHOLE],
        out_specs=pl.BlockSpec((LT * 8, 128), lambda i: (i, 0)),
        out_shape=pltpu.HBM((8192, 128), BF),
        scratch_shapes=[pltpu.VMEM((2, 512, 2048), BF), pltpu.VMEM((LT * LP, 128), F32)],
        name="angular",
        compiler_params=pltpu.CompilerParams(vmem_limit_bytes=24 << 20),
        cost_estimate=cost(2 * 1024 * 2048 * 1024, 14 << 20),
    )(r, leg)


def spread_kernel(bes_ref, o_ref):
    src = lax.broadcasted_iota(jnp.int32, (256, 1024), 0)
    lam = lax.broadcasted_iota(jnp.int32, (256, 1024), 1)
    shell = (lam // 128) * 32 + 2 * (lam % 16) + (lam // 64) % 2
    one = jnp.where(src == shell, 1.0, 0.0).astype(BF)
    o_ref[...] = lax.dot_general(bes_ref[...], one, NN, preferred_element_type=F32).astype(BF)


def spread(bes):
    return pl.pallas_call(
        spread_kernel,
        in_specs=[WHOLE],
        out_specs=WHOLE,
        out_shape=jax.ShapeDtypeStruct((512, 1024), BF),
        name="spread",
        compiler_params=pltpu.CompilerParams(vmem_limit_bytes=8 << 20),
        cost_estimate=cost(2 * 512 * 256 * 1024, 2 << 20),
    )(bes)


def radial_kernel(r_ref, wide_ref, o_ref, f32s, weight, held):
    l = pl.program_id(0)

    @pl.when(l == 0)
    def _():
        f32s[...] = r_ref[...].astype(F32)

    field = (lax.broadcasted_iota(jnp.int32, (128, 1024), 1) // 16) % 4
    tiled = wide_ref[...]
    for f in range(4):
        weight[f * 128 : (f + 1) * 128, :] = jnp.where(field == f, tiled, jnp.zeros_like(tiled))
    for n in range(8):
        for q in range(8):
            held[n * 32 : (n + 1) * 32, q * 128 : (q + 1) * 128] = f32s[
                pl.ds(q * 32 + l * 8 + n, 32, stride=256), :
            ].astype(BF)
    y = lax.dot_general(held[...], weight[...], NT, preferred_element_type=F32)
    for n in range(8):
        p, fh = n // 2, n % 2
        for f in range(4):
            o_ref[0, fh * 4 + f, pl.ds(p, 32, stride=4), :] = y[n * 32 : (n + 1) * 32, f * 128 : (f + 1) * 128]


def radial(r, wide):
    return pl.pallas_call(
        radial_kernel,
        grid=(4,),
        in_specs=[WHOLE, pl.BlockSpec((128, 1024), lambda i: (i, 0))],
        out_specs=pl.BlockSpec((1, 8, 128, 128), lambda i: (i, 0, 0, 0)),
        out_shape=jax.ShapeDtypeStruct((4, 8, 128, 128), F32),
        scratch_shapes=[pltpu.VMEM((8192, 128), F32), pltpu.VMEM((512, 1024), BF), pltpu.VMEM((256, 1024), BF)],
        name="radial",
        compiler_params=pltpu.CompilerParams(vmem_limit_bytes=20 << 20),
        cost_estimate=cost(2 * 4 * 256 * 1024 * 512, 5 << 20),
    )(r, wide)


def on_device(spectra, selection, legendre, bessel, order_perm):
    x = jnp.transpose(spectra, (1, 2, 3, 0)).reshape(8, 2048, 128)
    x = pltpu.with_memory_space_constraint(x, pltpu.HBM)
    w = weigh(pltpu.with_memory_space_constraint(order_perm.reshape(1, 64), pltpu.HBM), pltpu.with_memory_space_constraint(selection, pltpu.HBM), x).reshape(32, 512, 128)
    w = lax.all_to_all(w, "blk", split_axis=0, concat_axis=0, tiled=True)
    wide = spread(bessel.reshape(512, 256))
    h = angular(w, legendre).reshape(256, 32, 128)
    h = lax.all_to_all(h, ("blk", "shell"), split_axis=0, concat_axis=0, tiled=True)
    return radial(h.reshape(8192, 128), wide)


def solution(mesh):
    in_specs = (
        P(None, None, "shell", "blk"),
        P("shell", "blk"),
        P("blk", None, None),
        P(("blk", "shell"), None, None),
        P(),
    )
    out_specs = P(("blk", "shell"), None, None, None)
    return jax.shard_map(
        on_device, mesh=mesh, in_specs=in_specs, out_specs=out_specs, check_vma=False
    )
```

```python
import functools
import jax
import jax.numpy as jnp
from jax import lax
from jax.experimental import pallas as pl
from jax.experimental.pallas import tpu as pltpu
from jax.sharding import PartitionSpec as P

NT = (((1,), (1,)), ((), ()))
NN = (((1,), (0,)), ((), ()))
BF = jnp.bfloat16
F32 = jnp.float32
WHOLE = pl.BlockSpec(memory_space=pltpu.VMEM)


def cost(flops, moved):
    return pl.CostEstimate(flops=flops, bytes_accessed=moved, transcendentals=0)


FS = 4


def onehot(rows, where):
    row = lax.broadcasted_iota(jnp.int32, (rows, rows), 0)
    col = lax.broadcasted_iota(jnp.int32, (rows, rows), 1)
    return jnp.where(where(row) == col, 1.0, 0.0).astype(BF)


def weigh_kernel(perm_ref, sel_ref, x_ref, o_ref, pair, pick_ref, swap):
    @pl.when(pl.program_id(0) == 0)
    def _():
        for rp in range(16):
            pair[:, rp * 128 : (rp + 1) * 128] = jnp.concatenate(
                [sel_ref[2 * rp : 2 * rp + 1, :], sel_ref[2 * rp + 1 : 2 * rp + 2, :]], axis=1
            )
        p = lax.broadcasted_iota(jnp.int32, (128, 64), 0)
        lane = lax.broadcasted_iota(jnp.int32, (128, 64), 1)
        held = jnp.sum(jnp.where(p // 2 == lane, 2 * perm_ref[...] + p % 2, 0), axis=1, keepdims=True)
        col = lax.broadcasted_iota(jnp.int32, (128, 128), 1)
        pick_ref[...] = jnp.where(held == col, 1.0, 0.0).astype(BF)
        swap[...] = onehot(256, lambda i: i % 16 * 16 + i // 16)

    for t in range(FS):
        f = pl.program_id(0) * FS + t
        ws = []
        for g in range(8):
            y = lax.dot_general(
                pick_ref[...], x_ref[t, g * 256 : (g + 1) * 256, :], NT, preferred_element_type=F32
            )
            ws.append((y * pair[:, g * 256 : (g + 1) * 256]).astype(BF))
        for k in range(0, 8, 2):
            rows = jnp.concatenate(
                [
                    jnp.concatenate(
                        [ws[rp // 2][(k + h) * 16 : (k + h + 1) * 16, rp % 2 * 128 : rp % 2 * 128 + 128] for h in range(2)],
                        axis=1,
                    )
                    for rp in range(16)
                ],
                axis=0,
            )
            out = lax.dot_general(swap[...], rows, NN, preferred_element_type=F32).astype(BF)
            for h in range(2):
                o_ref[(k + h) * 16 : (k + h + 1) * 16, f, :, :] = out[:, h * 128 : (h + 1) * 128].reshape(16, 16, 128)


def weigh(perm, sel, x):
    return pl.pallas_call(
        weigh_kernel,
        grid=(8 // FS,),
        in_specs=[
            pl.BlockSpec((1, 64), lambda i: (0, 0)),
            pl.BlockSpec((32, 64), lambda i: (0, 0)),
            pl.BlockSpec((FS, 2048, 128), lambda i: (i, 0, 0)),
        ],
        out_specs=WHOLE,
        out_shape=jax.ShapeDtypeStruct((128, 8, 16, 128), BF),
        scratch_shapes=[pltpu.VMEM((1, 2048), F32), pltpu.VMEM((128, 128), BF), pltpu.VMEM((256, 256), BF)],
        name="weigh",
        compiler_params=pltpu.CompilerParams(vmem_limit_bytes=20 << 20),
        cost_estimate=cost(2 * 16384 * 128 * 128, 8 << 20),
    )(perm, sel, x)


LT = 1024


def angular_kernel(r_ref, leg_ref, o_ref, lhs, scr):
    @pl.when(pl.program_id(0) == 0)
    def _():
        for p in range(4):
            s, c = p // 2, p % 2
            for fh in range(2):
                rows = slice(p * 128 + fh * 64, p * 128 + fh * 64 + 64)
                to = c * 256 + fh * 128
                for g in range(16):
                    a = r_ref[2 * g, rows, :]
                    b = r_ref[2 * g + 1, rows, :]
                    ks = slice(g * 128, (g + 1) * 128)
                    lhs[s, to : to + 64, ks] = jnp.concatenate([a[:, :64], b[:, :64]], axis=1)
                    lhs[s, to + 64 : to + 128, ks] = jnp.concatenate([a[:, 64:], b[:, 64:]], axis=1)

    for s in range(2):
        h = lax.dot_general(lhs[s], leg_ref[s, :, pl.ds(pl.multiple_of(pl.program_id(0) * LT, LT), LT)], NN, preferred_element_type=F32)
        ht = h.T
        for n in range(4):
            scr[pl.ds(4 * s + n, LT, stride=8), :] = ht[:, n * 128 : (n + 1) * 128]
    o_ref[...] = scr[...].astype(BF)


def angular(r, leg):
    return pl.pallas_call(
        angular_kernel,
        grid=(1024 // LT,),
        in_specs=[WHOLE, WHOLE],
        out_specs=pl.BlockSpec((LT * 8, 128), lambda i: (i, 0)),
        out_shape=pltpu.HBM((8192, 128), BF),
        scratch_shapes=[pltpu.VMEM((2, 512, 2048), BF), pltpu.VMEM((LT * 8, 128), F32)],
        name="angular",
        compiler_params=pltpu.CompilerParams(vmem_limit_bytes=24 << 20),
        cost_estimate=cost(2 * 1024 * 2048 * 1024, 14 << 20),
    )(r, leg)


def spread_kernel(bes_ref, o_ref):
    src = lax.broadcasted_iota(jnp.int32, (256, 1024), 0)
    lam = lax.broadcasted_iota(jnp.int32, (256, 1024), 1)
    shell = (lam // 128) * 32 + 2 * (lam % 16) + (lam // 64) % 2
    one = jnp.where(src == shell, 1.0, 0.0).astype(BF)
    o_ref[...] = lax.dot_general(bes_ref[...], one, NN, preferred_element_type=F32).astype(BF)


def spread(bes):
    return pl.pallas_call(
        spread_kernel,
        in_specs=[WHOLE],
        out_specs=WHOLE,
        out_shape=jax.ShapeDtypeStruct((512, 1024), BF),
        name="spread",
        compiler_params=pltpu.CompilerParams(vmem_limit_bytes=8 << 20),
        cost_estimate=cost(2 * 512 * 256 * 1024, 2 << 20),
    )(bes)


def radial_kernel(r_ref, wide_ref, o_ref, held, weight):
    l = pl.program_id(0)

    @pl.when(l == 0)
    def _():
        swap = onehot(128, lambda i: i % 16 // 4 * 32 + i // 16 % 4 * 8 + i % 4 * 2 + i // 64)
        for g in range(8):
            rows = jnp.concatenate(
                [
                    jnp.concatenate(
                        [r_ref[(b * 8 + q) * 32 : (b * 8 + q) * 32 + 32, :] for b in range(g * 4, g * 4 + 4)], axis=0
                    )
                    for q in range(8)
                ],
                axis=1,
            )
            out = lax.dot_general(swap, rows, NN, preferred_element_type=F32).astype(BF)
            for fh in range(2):
                for n in range(4):
                    at = (fh * 4 + n) * 16
                    held[n, fh * 128 + g * 16 : fh * 128 + g * 16 + 16, :] = out[at : at + 16, :]

    field = (lax.broadcasted_iota(jnp.int32, (128, 1024), 1) // 16) % 4
    tiled = wide_ref[...]
    for f in range(4):
        weight[f * 128 : (f + 1) * 128, :] = jnp.where(field == f, tiled, jnp.zeros_like(tiled))
    y = lax.dot_general(held[l], weight[...], NT, preferred_element_type=F32)
    for fh in range(2):
        for f in range(4):
            o_ref[0, fh * 4 + f, :, :] = y[fh * 128 : (fh + 1) * 128, f * 128 : (f + 1) * 128]


def radial(r, wide):
    return pl.pallas_call(
        radial_kernel,
        grid=(4,),
        in_specs=[WHOLE, pl.BlockSpec((128, 1024), lambda i: (i, 0))],
        out_specs=pl.BlockSpec((1, 8, 128, 128), lambda i: (i, 0, 0, 0)),
        out_shape=jax.ShapeDtypeStruct((4, 8, 128, 128), F32),
        scratch_shapes=[pltpu.VMEM((4, 256, 1024), BF), pltpu.VMEM((512, 1024), BF)],
        name="radial",
        compiler_params=pltpu.CompilerParams(vmem_limit_bytes=20 << 20),
        cost_estimate=cost(2 * 4 * 256 * 1024 * 512, 5 << 20),
    )(r, wide)


def on_device(spectra, selection, legendre, bessel, order_perm):
    x = jnp.transpose(spectra, (1, 2, 3, 0)).reshape(8, 2048, 128)
    x = pltpu.with_memory_space_constraint(x, pltpu.HBM)
    w = weigh(pltpu.with_memory_space_constraint(order_perm.reshape(1, 64), pltpu.HBM), pltpu.with_memory_space_constraint(selection, pltpu.HBM), x).reshape(32, 512, 128)
    w = lax.all_to_all(w, "blk", split_axis=0, concat_axis=0, tiled=True)
    wide = spread(bessel.reshape(512, 256))
    h = angular(w, legendre).reshape(256, 32, 128)
    h = lax.all_to_all(h, ("blk", "shell"), split_axis=0, concat_axis=0, tiled=True)
    return radial(h.reshape(8192, 128), wide)


def solution(mesh):
    in_specs = (
        P(None, None, "shell", "blk"),
        P("shell", "blk"),
        P("blk", None, None),
        P(("blk", "shell"), None, None),
        P(),
    )
    out_specs = P(("blk", "shell"), None, None, None)
    return jax.shard_map(
        on_device, mesh=mesh, in_specs=in_specs, out_specs=out_specs, check_vma=False
    )
```

```python
import functools
import jax
import jax.numpy as jnp
from jax import lax
from jax.experimental import pallas as pl
from jax.experimental.pallas import tpu as pltpu
from jax.sharding import PartitionSpec as P

NT = (((1,), (1,)), ((), ()))
NN = (((1,), (0,)), ((), ()))
BF = jnp.bfloat16
F32 = jnp.float32
WHOLE = pl.BlockSpec(memory_space=pltpu.VMEM)


def cost(flops, moved):
    return pl.CostEstimate(flops=flops, bytes_accessed=moved, transcendentals=0)


FS = 4


def onehot(rows, where):
    row = lax.broadcasted_iota(jnp.int32, (rows, rows), 0)
    col = lax.broadcasted_iota(jnp.int32, (rows, rows), 1)
    return jnp.where(where(row) == col, 1.0, 0.0).astype(BF)


def weigh_kernel(perm_ref, sel_ref, x_ref, o_ref, pair, pick_ref, swap):
    @pl.when(pl.program_id(0) == 0)
    def _():
        for rp in range(16):
            pair[:, rp * 128 : (rp + 1) * 128] = jnp.concatenate(
                [sel_ref[2 * rp : 2 * rp + 1, :], sel_ref[2 * rp + 1 : 2 * rp + 2, :]], axis=1
            )
        p = lax.broadcasted_iota(jnp.int32, (128, 64), 0)
        lane = lax.broadcasted_iota(jnp.int32, (128, 64), 1)
        held = jnp.sum(jnp.where(p // 2 == lane, 2 * perm_ref[...] + p % 2, 0), axis=1, keepdims=True)
        col = lax.broadcasted_iota(jnp.int32, (128, 128), 1)
        pick_ref[...] = jnp.where(held == col, 1.0, 0.0).astype(BF)
        swap[...] = onehot(256, lambda i: i % 16 * 16 + i // 16)

    for t in range(FS):
        f = pl.program_id(0) * FS + t
        ws = []
        for g in range(8):
            y = lax.dot_general(
                pick_ref[...], x_ref[t, g * 256 : (g + 1) * 256, :], NT, preferred_element_type=F32
            )
            ws.append((y * pair[:, g * 256 : (g + 1) * 256]).astype(BF))
        for k in range(0, 8, 2):
            rows = jnp.concatenate(
                [
                    jnp.concatenate(
                        [ws[rp // 2][(k + h) * 16 : (k + h + 1) * 16, rp % 2 * 128 : rp % 2 * 128 + 128] for h in range(2)],
                        axis=1,
                    )
                    for rp in range(16)
                ],
                axis=0,
            )
            out = lax.dot_general(swap[...], rows, NN, preferred_element_type=F32).astype(BF)
            for h in range(2):
                o_ref[(k + h) * 16 : (k + h + 1) * 16, f, :, :] = out[:, h * 128 : (h + 1) * 128].reshape(16, 16, 128)


def weigh(perm, sel, x):
    return pl.pallas_call(
        weigh_kernel,
        grid=(8 // FS,),
        in_specs=[
            pl.BlockSpec((1, 64), lambda i: (0, 0)),
            pl.BlockSpec((32, 64), lambda i: (0, 0)),
            pl.BlockSpec((FS, 2048, 128), lambda i: (i, 0, 0)),
        ],
        out_specs=WHOLE,
        out_shape=jax.ShapeDtypeStruct((128, 8, 16, 128), BF),
        scratch_shapes=[pltpu.VMEM((1, 2048), F32), pltpu.VMEM((128, 128), BF), pltpu.VMEM((256, 256), BF)],
        name="weigh",
        compiler_params=pltpu.CompilerParams(vmem_limit_bytes=20 << 20),
        cost_estimate=cost(2 * 16384 * 128 * 128, 8 << 20),
    )(perm, sel, x)


LT = 1024


def angular_kernel(r_ref, leg_ref, o_ref, lhs, scr):
    @pl.when(pl.program_id(0) == 0)
    def _():
        for p in range(4):
            s, c = p // 2, p % 2
            for fh in range(2):
                rows = slice(p * 128 + fh * 64, p * 128 + fh * 64 + 64)
                to = c * 256 + fh * 128
                for g in range(16):
                    a = r_ref[2 * g, rows, :]
                    b = r_ref[2 * g + 1, rows, :]
                    ks = slice(g * 128, (g + 1) * 128)
                    lhs[s, to : to + 64, ks] = jnp.concatenate([a[:, :64], b[:, :64]], axis=1)
                    lhs[s, to + 64 : to + 128, ks] = jnp.concatenate([a[:, 64:], b[:, 64:]], axis=1)

    for s in range(2):
        h = lax.dot_general(lhs[s], leg_ref[s, :, pl.ds(pl.multiple_of(pl.program_id(0) * LT, LT), LT)], NN, preferred_element_type=F32)
        ht = h.T
        for n in range(4):
            scr[pl.ds(4 * s + n, LT, stride=8), :] = ht[:, n * 128 : (n + 1) * 128]
    o_ref[...] = scr[...].astype(BF)


def angular(r, leg):
    return pl.pallas_call(
        angular_kernel,
        grid=(1024 // LT,),
        in_specs=[WHOLE, WHOLE],
        out_specs=WHOLE,
        out_shape=jax.ShapeDtypeStruct((8192, 128), BF),
        scratch_shapes=[pltpu.VMEM((2, 512, 2048), BF), pltpu.VMEM((LT * 8, 128), F32)],
        name="angular",
        compiler_params=pltpu.CompilerParams(vmem_limit_bytes=24 << 20),
        cost_estimate=cost(2 * 1024 * 2048 * 1024, 14 << 20),
    )(r, leg)


def radial_kernel(r_ref, bes_ref, o_ref, held, weight, spread):
    l = pl.program_id(0)

    @pl.when(l == 0)
    def _():
        swap = onehot(128, lambda i: i % 16 // 4 * 32 + i // 16 % 4 * 8 + i % 4 * 2 + i // 64)
        for g in range(8):
            rows = jnp.concatenate(
                [
                    jnp.concatenate(
                        [r_ref[(b * 8 + q) * 32 : (b * 8 + q) * 32 + 32, :] for b in range(g * 4, g * 4 + 4)], axis=0
                    )
                    for q in range(8)
                ],
                axis=1,
            )
            out = lax.dot_general(swap, rows, NN, preferred_element_type=F32).astype(BF)
            for fh in range(2):
                for n in range(4):
                    at = (fh * 4 + n) * 16
                    held[n, fh * 128 + g * 16 : fh * 128 + g * 16 + 16, :] = out[at : at + 16, :]

        src = lax.broadcasted_iota(jnp.int32, (256, 1024), 0)
        lam = lax.broadcasted_iota(jnp.int32, (256, 1024), 1)
        shell = (lam // 128) * 32 + 2 * (lam % 16) + (lam // 64) % 2
        spread[...] = jnp.where(src == shell, 1.0, 0.0).astype(BF)

    field = (lax.broadcasted_iota(jnp.int32, (128, 1024), 1) // 16) % 4
    tiled = lax.dot_general(bes_ref[0], spread[...], NN, preferred_element_type=F32).astype(BF)
    for f in range(4):
        weight[f * 128 : (f + 1) * 128, :] = jnp.where(field == f, tiled, jnp.zeros_like(tiled))
    y = lax.dot_general(held[l], weight[...], NT, preferred_element_type=F32)
    for fh in range(2):
        for f in range(4):
            o_ref[0, fh * 4 + f, :, :] = y[fh * 128 : (fh + 1) * 128, f * 128 : (f + 1) * 128]


def radial(r, bes):
    return pl.pallas_call(
        radial_kernel,
        grid=(4,),
        in_specs=[WHOLE, pl.BlockSpec((1, 128, 256), lambda i: (i, 0, 0))],
        out_specs=pl.BlockSpec((1, 8, 128, 128), lambda i: (i, 0, 0, 0)),
        out_shape=jax.ShapeDtypeStruct((4, 8, 128, 128), F32),
        scratch_shapes=[pltpu.VMEM((4, 256, 1024), BF), pltpu.VMEM((512, 1024), BF), pltpu.VMEM((256, 1024), BF)],
        name="radial",
        compiler_params=pltpu.CompilerParams(vmem_limit_bytes=20 << 20),
        cost_estimate=cost(2 * 4 * 256 * 1024 * 512, 5 << 20),
    )(r, bes)


def on_device(spectra, selection, legendre, bessel, order_perm):
    x = jnp.transpose(spectra, (1, 2, 3, 0)).reshape(8, 2048, 128)
    x = pltpu.with_memory_space_constraint(x, pltpu.HBM)
    w = weigh(pltpu.with_memory_space_constraint(order_perm.reshape(1, 64), pltpu.HBM), pltpu.with_memory_space_constraint(selection, pltpu.HBM), x).reshape(32, 512, 128)
    w = lax.all_to_all(w, "blk", split_axis=0, concat_axis=0, tiled=True)
    h = angular(w, legendre).reshape(256, 32, 128)
    h = lax.all_to_all(h, ("blk", "shell"), split_axis=0, concat_axis=0, tiled=True)
    return radial(h.reshape(8192, 128), bessel)


def solution(mesh):
    in_specs = (
        P(None, None, "shell", "blk"),
        P("shell", "blk"),
        P("blk", None, None),
        P(("blk", "shell"), None, None),
        P(),
    )
    out_specs = P(("blk", "shell"), None, None, None)
    return jax.shard_map(
        on_device, mesh=mesh, in_specs=in_specs, out_specs=out_specs, check_vma=False
    )
```

```python
import functools
import jax
import jax.numpy as jnp
from jax import lax
from jax.experimental import pallas as pl
from jax.experimental.pallas import tpu as pltpu
from jax.sharding import PartitionSpec as P

NT = (((1,), (1,)), ((), ()))
NN = (((1,), (0,)), ((), ()))
BF = jnp.bfloat16
F32 = jnp.float32
WHOLE = pl.BlockSpec(memory_space=pltpu.VMEM)


def cost(flops, moved):
    return pl.CostEstimate(flops=flops, bytes_accessed=moved, transcendentals=0)


FS = 4


def onehot(rows, where):
    row = lax.broadcasted_iota(jnp.int32, (rows, rows), 0)
    col = lax.broadcasted_iota(jnp.int32, (rows, rows), 1)
    return jnp.where(where(row) == col, 1.0, 0.0).astype(BF)


def weigh_kernel(perm_ref, sel_ref, x_ref, o_ref, pair, pick_ref, swap):
    @pl.when(pl.program_id(0) == 0)
    def _():
        for rp in range(16):
            pair[:, rp * 128 : (rp + 1) * 128] = jnp.concatenate(
                [sel_ref[2 * rp : 2 * rp + 1, :], sel_ref[2 * rp + 1 : 2 * rp + 2, :]], axis=1
            )
        p = lax.broadcasted_iota(jnp.int32, (128, 64), 0)
        lane = lax.broadcasted_iota(jnp.int32, (128, 64), 1)
        held = jnp.sum(jnp.where(p // 2 == lane, 2 * perm_ref[...] + p % 2, 0), axis=1, keepdims=True)
        col = lax.broadcasted_iota(jnp.int32, (128, 128), 1)
        pick_ref[...] = jnp.where(held == col, 1.0, 0.0).astype(BF)
        swap[...] = onehot(256, lambda i: i % 16 * 16 + i // 16)

    for t in range(FS):
        f = pl.program_id(0) * FS + t
        ws = []
        for g in range(8):
            y = lax.dot_general(
                pick_ref[...], x_ref[t, g * 256 : (g + 1) * 256, :], NT, preferred_element_type=F32
            )
            ws.append((y * pair[:, g * 256 : (g + 1) * 256]).astype(BF))
        for k in range(0, 8, 2):
            rows = jnp.concatenate(
                [
                    jnp.concatenate(
                        [ws[rp // 2][(k + h) * 16 : (k + h + 1) * 16, rp % 2 * 128 : rp % 2 * 128 + 128] for h in range(2)],
                        axis=1,
                    )
                    for rp in range(16)
                ],
                axis=0,
            )
            out = lax.dot_general(swap[...], rows, NN, preferred_element_type=F32).astype(BF)
            for h in range(2):
                o_ref[(k + h) * 16 : (k + h + 1) * 16, f, :, :] = out[:, h * 128 : (h + 1) * 128].reshape(16, 16, 128)


def weigh(perm, sel, x):
    return pl.pallas_call(
        weigh_kernel,
        grid=(8 // FS,),
        in_specs=[
            pl.BlockSpec((1, 64), lambda i: (0, 0)),
            pl.BlockSpec((32, 64), lambda i: (0, 0)),
            pl.BlockSpec((FS, 2048, 128), lambda i: (i, 0, 0)),
        ],
        out_specs=WHOLE,
        out_shape=jax.ShapeDtypeStruct((128, 8, 16, 128), BF),
        scratch_shapes=[pltpu.VMEM((1, 2048), F32), pltpu.VMEM((128, 128), BF), pltpu.VMEM((256, 256), BF)],
        name="weigh",
        compiler_params=pltpu.CompilerParams(vmem_limit_bytes=20 << 20),
        cost_estimate=cost(2 * 16384 * 128 * 128, 8 << 20),
    )(perm, sel, x)


LT = 1024


def angular_kernel(r_ref, leg_ref, o_ref, lhs, scr):
    @pl.when(pl.program_id(0) == 0)
    def _():
        for p in range(4):
            s, c = p // 2, p % 2
            for fh in range(2):
                rows = slice(p * 128 + fh * 64, p * 128 + fh * 64 + 64)
                to = c * 256 + fh * 128
                for g in range(16):
                    a = r_ref[2 * g, rows, :]
                    b = r_ref[2 * g + 1, rows, :]
                    ks = slice(g * 128, (g + 1) * 128)
                    lhs[s, to : to + 64, ks] = jnp.concatenate([a[:, :64], b[:, :64]], axis=1)
                    lhs[s, to + 64 : to + 128, ks] = jnp.concatenate([a[:, 64:], b[:, 64:]], axis=1)

    for s in range(2):
        h = lax.dot_general(lhs[s], leg_ref[s, :, pl.ds(pl.multiple_of(pl.program_id(0) * LT, LT), LT)], NN, preferred_element_type=F32)
        ht = h.T
        for n in range(4):
            scr[pl.ds(4 * s + n, LT, stride=8), :] = ht[:, n * 128 : (n + 1) * 128]
    o_ref[...] = scr[...].astype(BF)


def angular(r, leg):
    return pl.pallas_call(
        angular_kernel,
        grid=(1024 // LT,),
        in_specs=[WHOLE, WHOLE],
        out_specs=WHOLE,
        out_shape=jax.ShapeDtypeStruct((8192, 128), BF),
        scratch_shapes=[pltpu.VMEM((2, 512, 2048), BF), pltpu.VMEM((LT * 8, 128), F32)],
        name="angular",
        compiler_params=pltpu.CompilerParams(vmem_limit_bytes=24 << 20),
        cost_estimate=cost(2 * 1024 * 2048 * 1024, 14 << 20),
    )(r, leg)


def radial_kernel(r_ref, bes_ref, o_ref, held, weight, spread):
    l = pl.program_id(0)

    @pl.when(l == 0)
    def _():
        swap = onehot(128, lambda i: i % 16 // 4 * 32 + i // 16 % 4 * 8 + i % 4 * 2 + i // 64)
        for g in range(8):
            rows = jnp.concatenate(
                [
                    jnp.concatenate(
                        [r_ref[(b * 8 + q) * 32 : (b * 8 + q) * 32 + 32, :] for b in range(g * 4, g * 4 + 4)], axis=0
                    )
                    for q in range(8)
                ],
                axis=1,
            )
            out = lax.dot_general(swap, rows, NN, preferred_element_type=F32).astype(BF)
            for fh in range(2):
                for n in range(4):
                    at = (fh * 4 + n) * 16
                    held[n, fh * 128 + g * 16 : fh * 128 + g * 16 + 16, :] = out[at : at + 16, :]

        src = lax.broadcasted_iota(jnp.int32, (256, 1024), 0)
        lam = lax.broadcasted_iota(jnp.int32, (256, 1024), 1)
        shell = (lam // 128) * 32 + 2 * (lam % 16) + (lam // 64) % 2
        spread[...] = jnp.where(src == shell, 1.0, 0.0).astype(BF)

    field = (lax.broadcasted_iota(jnp.int32, (128, 1024), 1) // 16) % 4
    for t in range(2):
        tiled = lax.dot_general(bes_ref[t], spread[...], NN, preferred_element_type=F32).astype(BF)
        for f in range(4):
            weight[f * 128 : (f + 1) * 128, :] = jnp.where(field == f, tiled, jnp.zeros_like(tiled))
        y = lax.dot_general(held[2 * l + t], weight[...], NT, preferred_element_type=F32)
        for fh in range(2):
            for f in range(4):
                o_ref[t, fh * 4 + f, :, :] = y[fh * 128 : (fh + 1) * 128, f * 128 : (f + 1) * 128]


def radial(r, bes):
    return pl.pallas_call(
        radial_kernel,
        grid=(2,),
        in_specs=[WHOLE, pl.BlockSpec((2, 128, 256), lambda i: (i, 0, 0))],
        out_specs=pl.BlockSpec((2, 8, 128, 128), lambda i: (i, 0, 0, 0)),
        out_shape=jax.ShapeDtypeStruct((4, 8, 128, 128), F32),
        scratch_shapes=[pltpu.VMEM((4, 256, 1024), BF), pltpu.VMEM((512, 1024), BF), pltpu.VMEM((256, 1024), BF)],
        name="radial",
        compiler_params=pltpu.CompilerParams(vmem_limit_bytes=20 << 20),
        cost_estimate=cost(2 * 4 * 256 * 1024 * 512, 5 << 20),
    )(r, bes)


def on_device(spectra, selection, legendre, bessel, order_perm):
    x = jnp.transpose(spectra, (1, 2, 3, 0)).reshape(8, 2048, 128)
    x = pltpu.with_memory_space_constraint(x, pltpu.HBM)
    w = weigh(pltpu.with_memory_space_constraint(order_perm.reshape(1, 64), pltpu.HBM), pltpu.with_memory_space_constraint(selection, pltpu.HBM), x).reshape(32, 512, 128)
    w = lax.all_to_all(w, "blk", split_axis=0, concat_axis=0, tiled=True)
    h = angular(w, legendre).reshape(256, 32, 128)
    h = lax.all_to_all(h, ("blk", "shell"), split_axis=0, concat_axis=0, tiled=True)
    return radial(h.reshape(8192, 128), bessel)


def solution(mesh):
    in_specs = (
        P(None, None, "shell", "blk"),
        P("shell", "blk"),
        P("blk", None, None),
        P(("blk", "shell"), None, None),
        P(),
    )
    out_specs = P(("blk", "shell"), None, None, None)
    return jax.shard_map(
        on_device, mesh=mesh, in_specs=in_specs, out_specs=out_specs, check_vma=False
    )
```

```python
import functools
import jax
import jax.numpy as jnp
from jax import lax
from jax.experimental import pallas as pl
from jax.experimental.pallas import tpu as pltpu
from jax.sharding import PartitionSpec as P

NT = (((1,), (1,)), ((), ()))
NN = (((1,), (0,)), ((), ()))
BF = jnp.bfloat16
F32 = jnp.float32
WHOLE = pl.BlockSpec(memory_space=pltpu.VMEM)


def cost(flops, moved):
    return pl.CostEstimate(flops=flops, bytes_accessed=moved, transcendentals=0)


FS = 4


def onehot(rows, where):
    row = lax.broadcasted_iota(jnp.int32, (rows, rows), 0)
    col = lax.broadcasted_iota(jnp.int32, (rows, rows), 1)
    return jnp.where(where(row) == col, 1.0, 0.0).astype(BF)


def weigh_kernel(perm_ref, sel_ref, x_ref, o_ref, pair, pick_ref, swap):
    @pl.when(pl.program_id(0) == 0)
    def _():
        for rp in range(16):
            pair[:, rp * 128 : (rp + 1) * 128] = jnp.concatenate(
                [sel_ref[2 * rp : 2 * rp + 1, :], sel_ref[2 * rp + 1 : 2 * rp + 2, :]], axis=1
            )
        p = lax.broadcasted_iota(jnp.int32, (128, 64), 0)
        lane = lax.broadcasted_iota(jnp.int32, (128, 64), 1)
        held = jnp.sum(jnp.where(p // 2 == lane, 2 * perm_ref[...] + p % 2, 0), axis=1, keepdims=True)
        col = lax.broadcasted_iota(jnp.int32, (128, 128), 1)
        pick_ref[...] = jnp.where(held == col, 1.0, 0.0).astype(BF)
        swap[...] = onehot(256, lambda i: i % 16 * 16 + i // 16)

    for t in range(FS):
        f = pl.program_id(0) * FS + t
        ws = []
        for g in range(8):
            y = lax.dot_general(
                pick_ref[...], x_ref[t, g * 256 : (g + 1) * 256, :], NT, preferred_element_type=F32
            )
            ws.append((y * pair[:, g * 256 : (g + 1) * 256]).astype(BF))
        for k in range(0, 8, 2):
            rows = jnp.concatenate(
                [
                    jnp.concatenate(
                        [ws[rp // 2][(k + h) * 16 : (k + h + 1) * 16, rp % 2 * 128 : rp % 2 * 128 + 128] for h in range(2)],
                        axis=1,
                    )
                    for rp in range(16)
                ],
                axis=0,
            )
            out = lax.dot_general(swap[...], rows, NN, preferred_element_type=F32).astype(BF)
            for h in range(2):
                o_ref[(k + h) * 16 : (k + h + 1) * 16, f, :, :] = out[:, h * 128 : (h + 1) * 128].reshape(16, 16, 128)


def weigh(perm, sel, x):
    return pl.pallas_call(
        weigh_kernel,
        grid=(8 // FS,),
        in_specs=[
            pl.BlockSpec((1, 64), lambda i: (0, 0)),
            pl.BlockSpec((32, 64), lambda i: (0, 0)),
            pl.BlockSpec((FS, 2048, 128), lambda i: (i, 0, 0)),
        ],
        out_specs=WHOLE,
        out_shape=jax.ShapeDtypeStruct((128, 8, 16, 128), BF),
        scratch_shapes=[pltpu.VMEM((1, 2048), F32), pltpu.VMEM((128, 128), BF), pltpu.VMEM((256, 256), BF)],
        name="weigh",
        compiler_params=pltpu.CompilerParams(vmem_limit_bytes=20 << 20),
        cost_estimate=cost(2 * 16384 * 128 * 128, 8 << 20),
    )(perm, sel, x)


LT = 1024


def angular_kernel(r_ref, leg_ref, o_ref, lhs, scr):
    @pl.when(pl.program_id(0) == 0)
    def _():
        for p in range(4):
            s, c = p // 2, p % 2
            for fh in range(2):
                rows = slice(p * 128 + fh * 64, p * 128 + fh * 64 + 64)
                to = c * 256 + fh * 128
                for g in range(16):
                    a = r_ref[2 * g, rows, :]
                    b = r_ref[2 * g + 1, rows, :]
                    ks = slice(g * 128, (g + 1) * 128)
                    lhs[s, to : to + 64, ks] = jnp.concatenate([a[:, :64], b[:, :64]], axis=1)
                    lhs[s, to + 64 : to + 128, ks] = jnp.concatenate([a[:, 64:], b[:, 64:]], axis=1)

    for s in range(2):
        h = lax.dot_general(lhs[s], leg_ref[s, :, pl.ds(pl.multiple_of(pl.program_id(0) * LT, LT), LT)], NN, preferred_element_type=F32)
        ht = h.T
        for n in range(4):
            scr[pl.ds(4 * s + n, LT, stride=8), :] = ht[:, n * 128 : (n + 1) * 128]
    o_ref[...] = scr[...].astype(BF)


def angular(r, leg):
    return pl.pallas_call(
        angular_kernel,
        grid=(1024 // LT,),
        in_specs=[WHOLE, WHOLE],
        out_specs=WHOLE,
        out_shape=jax.ShapeDtypeStruct((8192, 128), BF),
        scratch_shapes=[pltpu.VMEM((2, 512, 2048), BF), pltpu.VMEM((LT * 8, 128), F32)],
        name="angular",
        compiler_params=pltpu.CompilerParams(vmem_limit_bytes=24 << 20),
        cost_estimate=cost(2 * 1024 * 2048 * 1024, 14 << 20),
    )(r, leg)


def radial_kernel(r_ref, bes_ref, o_ref, held, weight, spread):
    l = pl.program_id(0)

    @pl.when(l == 0)
    def _():
        swap = onehot(128, lambda i: i % 16 // 4 * 32 + i // 16 % 4 * 8 + i % 4 * 2 + i // 64)
        for g in range(8):
            rows = jnp.concatenate(
                [
                    jnp.concatenate(
                        [r_ref[(b * 8 + q) * 32 : (b * 8 + q) * 32 + 32, :] for b in range(g * 4, g * 4 + 4)], axis=0
                    )
                    for q in range(8)
                ],
                axis=1,
            )
            out = lax.dot_general(swap, rows, NN, preferred_element_type=F32).astype(BF)
            for fh in range(2):
                for n in range(4):
                    at = (fh * 4 + n) * 16
                    held[n, fh * 128 + g * 16 : fh * 128 + g * 16 + 16, :] = out[at : at + 16, :]

        src = lax.broadcasted_iota(jnp.int32, (256, 1024), 0)
        lam = lax.broadcasted_iota(jnp.int32, (256, 1024), 1)
        shell = (lam // 128) * 32 + 2 * (lam % 16) + (lam // 64) % 2
        spread[...] = jnp.where(src == shell, 1.0, 0.0).astype(BF)

    field = (lax.broadcasted_iota(jnp.int32, (128, 1024), 1) // 16) % 4
    pair = bes_ref[...].reshape(256, 256)
    both = lax.dot_general(pair, spread[...], NN, preferred_element_type=F32).astype(BF)
    for t in range(2):
        tiled = both[t * 128 : (t + 1) * 128, :]
        for f in range(4):
            weight[f * 128 : (f + 1) * 128, :] = jnp.where(field == f, tiled, jnp.zeros_like(tiled))
        y = lax.dot_general(held[2 * l + t], weight[...], NT, preferred_element_type=F32)
        for fh in range(2):
            for f in range(4):
                o_ref[t, fh * 4 + f, :, :] = y[fh * 128 : (fh + 1) * 128, f * 128 : (f + 1) * 128]


def radial(r, bes):
    return pl.pallas_call(
        radial_kernel,
        grid=(2,),
        in_specs=[WHOLE, pl.BlockSpec((2, 128, 256), lambda i: (i, 0, 0))],
        out_specs=pl.BlockSpec((2, 8, 128, 128), lambda i: (i, 0, 0, 0)),
        out_shape=jax.ShapeDtypeStruct((4, 8, 128, 128), F32),
        scratch_shapes=[pltpu.VMEM((4, 256, 1024), BF), pltpu.VMEM((512, 1024), BF), pltpu.VMEM((256, 1024), BF)],
        name="radial",
        compiler_params=pltpu.CompilerParams(vmem_limit_bytes=20 << 20),
        cost_estimate=cost(2 * 4 * 256 * 1024 * 512, 5 << 20),
    )(r, bes)


def on_device(spectra, selection, legendre, bessel, order_perm):
    x = jnp.transpose(spectra, (1, 2, 3, 0)).reshape(8, 2048, 128)
    x = pltpu.with_memory_space_constraint(x, pltpu.HBM)
    w = weigh(pltpu.with_memory_space_constraint(order_perm.reshape(1, 64), pltpu.HBM), pltpu.with_memory_space_constraint(selection, pltpu.HBM), x).reshape(32, 512, 128)
    w = lax.all_to_all(w, "blk", split_axis=0, concat_axis=0, tiled=True)
    h = angular(w, legendre).reshape(256, 32, 128)
    h = lax.all_to_all(h, ("blk", "shell"), split_axis=0, concat_axis=0, tiled=True)
    return radial(h.reshape(8192, 128), bessel)


def solution(mesh):
    in_specs = (
        P(None, None, "shell", "blk"),
        P("shell", "blk"),
        P("blk", None, None),
        P(("blk", "shell"), None, None),
        P(),
    )
    out_specs = P(("blk", "shell"), None, None, None)
    return jax.shard_map(
        on_device, mesh=mesh, in_specs=in_specs, out_specs=out_specs, check_vma=False
    )
```
